512 devices in a mesh: ca: 64 (over z, y), tp: 8 (over x, core).
Axes of the slice: x: 4, y: 4, z: 16, core: 2. Of those that a mesh axis runs over, the one named last changes fastest.
Arguments:
- tokens: bfloat16 [32768, 4096], P('ca'), may hold values from -7 to 7
- lengths: int32 [32], replicated, may hold values from 1 to 1536, 32768 in all
- w_query: bfloat16 [4096, 4096], P('ca', 'tp'), may hold values from -0.09375 to 0.09375
- w_key: bfloat16 [4096, 1024], P('ca', 'tp'), may hold values from -0.09375 to 0.09375
- w_value: bfloat16 [4096, 1024], P('ca', 'tp'), may hold values from -0.09375 to 0.09375
Outputs:
- attended: bfloat16 [32768, 4096], P('ca', 'tp')
The draws below stay inside these ranges and needn't reach their ends.
Inputs may be any that keep to these rules, and one draw needn't show every extreme that they name: `lengths`: the 32 documents lie end to end in this order and fill all 32768 tokens; the longest has exactly 1536 tokens.
All inputs are finite; a program needn't handle non-finite values.
Results may differ from the reference program's by a relative error of at most 0.007.
Values may be sent and summed in bfloat16 or wider, within the bound.
A program may use at most 64 MiB of HBM per device.

```python
import math
import jax
import jax.numpy as jnp
import numpy as np
from jax import lax

D = 4096
HEADS = 32
KV_HEADS = 8
HEAD_DIM = 128
TOK_DEV = 512
REACH = 3
TOKENS = 32768
MAX_DOC = 1536
DOCS = 32
N_CA = 64


def levels(rng, extent, pieces, least, largest):
    level = 1.0
    for position, parts in pieces:
        heights = jax.random.uniform(jax.random.fold_in(jax.random.fold_in(rng, 6), position), (parts,), jnp.float32, least / len(pieces), largest / len(pieces))
        level = level * jnp.repeat(jnp.exp(heights), extent[position] // parts).reshape((-1,) + (1,) * (len(extent) - 1 - position))
    return level


def length_profile(amount, total, limit, slope):
    portions = [(1 << 20) // math.isqrt(rank ** slope) + 1 for rank in range(2, amount + 1)]
    rest, given = total - limit - (amount - 1), [1] * (amount - 1)
    while rest > 0:
        movable = [i for i in range(amount - 1) if given[i] < limit]
        whole, remaining = sum([portions[i] for i in movable]), rest
        for i in movable:
            more = min(limit - given[i], max(1, remaining * portions[i] // whole), rest)
            given[i] = given[i] + more
            rest = rest - more
    return np.array([limit] + given)


def ragged_sizes(key, number_of, total, limit, slope):
    if number_of == 2:
        one = jax.random.randint(key, (), max(1, total - limit), min(limit, total - 1) + 1)
        return jnp.stack([one, total - one])
    sizes = jnp.asarray(length_profile(number_of, total, limit, slope), jnp.int32)
    couples = (number_of - 1) // 2
    donor, sink = sizes[1:1 + 2 * couples:2], sizes[2:2 + 2 * couples:2]
    room = jnp.minimum(donor - 1, limit - sink)
    passed = jax.random.randint(jax.random.fold_in(key, 1), (couples,), 0, 1 << 20) % (room + 1)
    sizes = sizes.at[1:1 + 2 * couples:2].set(donor - passed).at[2:2 + 2 * couples:2].set(sink + passed)
    return sizes[jax.random.permutation(jax.random.fold_in(key, 2), number_of)]


def centred(key, shape, deviation, limit, shards=(), held_as=jnp.bfloat16):
    entries = jax.random.normal(key, shape, jnp.float32) * deviation
    if len(shards) > 0:
        entries = levels(key, shape, shards, -0.22, 0.18) * entries
    return jnp.clip(entries, min=-limit, max=limit).astype(held_as)


def setup_inputs(seed: int = 0) -> dict:
    key_list = jax.random.split(jax.random.key(seed), 6)
    tokens = centred(key_list[0], (TOKENS, D), 1.2, 7.0, ((0, 64),))
    lengths = ragged_sizes(key_list[1], DOCS, TOKENS, MAX_DOC, 2).astype(jnp.int32)
    w_query = centred(key_list[2], (D, HEADS * HEAD_DIM), D ** -0.5, 0.09375, ((0, 64), (1, 8)))
    w_key = centred(key_list[3], (D, KV_HEADS * HEAD_DIM), D ** -0.5, 0.09375, ((0, 64), (1, 8)))
    w_value = centred(key_list[4], (D, KV_HEADS * HEAD_DIM), D ** -0.5, 0.09375, ((0, 64), (1, 8)))
    return {"tokens": tokens, "lengths": lengths, "w_query": w_query, "w_key": w_key, "w_value": w_value}


rope_theta = 500000.0
logit_cap = 5.0

def doc_starts(lengths, positions):
    doc_ends = jnp.cumsum(lengths).astype(jnp.int32)
    before = doc_ends[None, :] <= positions[:, None]
    return lax.optimization_barrier(jnp.max(jnp.where(before, doc_ends[None, :], jnp.zeros_like(doc_ends)[None, :]), axis=1)).astype(jnp.int32)

def rotate(values, offsets):
    half_dim = values.shape[-1] // 2
    frequency = rope_theta ** (-(jnp.arange(half_dim, dtype=jnp.float32) * 2.0) / values.shape[-1])
    angles = offsets.astype(jnp.float32)[:, None] * frequency[None, :]
    cosine = jnp.cos(angles)[:, None, :]
    sine_part = jnp.sin(angles)[:, None, :]
    first_half = values[..., :half_dim]
    second_half = values[..., half_dim:]
    return jnp.concatenate([first_half * cosine - second_half * sine_part, second_half * cosine + first_half * sine_part], axis=-1)

def reference(tokens, lengths, w_query, w_key, w_value):
    token_count = tokens.shape[0]
    row_ids = jnp.arange(token_count, dtype=jnp.int32)
    starts = doc_starts(lengths, row_ids)
    offsets = row_ids - starts
    query = jnp.dot(tokens, w_query, preferred_element_type=jnp.float32).reshape(token_count, HEADS, HEAD_DIM)
    query = rotate(query, offsets).astype(jnp.bfloat16)
    key_all = jnp.dot(tokens, w_key, preferred_element_type=jnp.float32).reshape(token_count, KV_HEADS, HEAD_DIM)
    key_all = rotate(key_all, offsets).astype(jnp.bfloat16)
    value_all = jnp.dot(tokens, w_value, preferred_element_type=jnp.float32).astype(jnp.bfloat16)
    value_all = value_all.reshape(token_count, KV_HEADS, HEAD_DIM)
    margin = REACH * TOK_DEV
    window = (REACH + 1) * TOK_DEV
    key_pad = jnp.concatenate([jnp.zeros((margin, KV_HEADS, HEAD_DIM), jnp.bfloat16), key_all], axis=0)
    value_pad = jnp.concatenate([jnp.zeros((margin, KV_HEADS, HEAD_DIM), jnp.bfloat16), value_all], axis=0)
    group_size = HEADS // KV_HEADS

    def one_block(block_index):
        first_row = (block_index * TOK_DEV).astype(jnp.int32)
        q_block = lax.dynamic_slice_in_dim(query, first_row, TOK_DEV, 0).astype(jnp.float32)
        q_block = q_block.reshape(TOK_DEV, KV_HEADS, group_size, HEAD_DIM)
        k_block = lax.dynamic_slice_in_dim(key_pad, first_row, window, 0).astype(jnp.float32)
        v_block = lax.dynamic_slice_in_dim(value_pad, first_row, window, 0).astype(jnp.float32)
        q_rows = first_row + jnp.arange(TOK_DEV, dtype=jnp.int32)
        k_rows = first_row - margin + jnp.arange(window, dtype=jnp.int32)
        q_starts = lax.dynamic_slice_in_dim(starts, first_row, TOK_DEV, 0)
        raw = jnp.einsum('tkgd,skd->kgts', q_block, k_block)
        scores = logit_cap * jnp.tanh(raw / (math.sqrt(HEAD_DIM) * logit_cap))
        allowed = (k_rows[None, :] <= q_rows[:, None]) & (k_rows[None, :] >= q_starts[:, None])
        weights = jnp.where(allowed[None, None], jnp.exp(scores), jnp.zeros_like(scores))
        totals = lax.optimization_barrier(jnp.sum(weights, axis=-1))
        rounded = lax.optimization_barrier(weights.astype(jnp.bfloat16)).astype(jnp.float32)
        mixed_out = jnp.einsum('kgts,skd->kgtd', rounded, v_block) / totals[..., None]
        mixed_out = jnp.transpose(mixed_out, (2, 0, 1, 3)).reshape(TOK_DEV, HEADS * HEAD_DIM)
        return mixed_out.astype(jnp.bfloat16)
    blocks = lax.map(one_block, jnp.arange(N_CA, dtype=jnp.int32))
    return blocks.reshape(token_count, HEADS * HEAD_DIM)
```

```python
import functools
import math

import jax
import jax.numpy as jnp
from jax import lax
from jax.experimental import pallas as pl
from jax.experimental.pallas import tpu as pltpu
from jax.sharding import PartitionSpec as P

GROUP = 4
HEAD_DIM = 128
TILE = 128
KEY_BLOCK = 256
REACH = 3
NY = 4

rope_theta = 500000.0
logit_cap = 5.0

MESH = pl.DeviceIdType.MESH


def doc_starts(lengths, positions):
    doc_ends = jnp.cumsum(lengths)
    before = doc_ends[None, :] <= positions[:, None]
    return jnp.max(jnp.where(before, doc_ends[None, :], jnp.zeros_like(doc_ends)[None, :]), axis=1)


def gather_kernel(
    nz,
    x_hbm, wq_hbm, wk_hbm, wv_hbm, cos_hbm, sin_hbm,
    q_out, win_out,
    xbuf, qbuf, kvbuf, accq, acckv, cosb, sinb, win,
    loc_sem, qz_s, qz_r, qy_s, qy_r, kz_s, kz_r, ky_s, ky_r, h_s, h_r, o_sem,
):
    n = nz * NY
    half = nz // 2
    rows = wq_hbm.shape[0]
    hr = rows // 2
    block = rows * NY
    c = lax.axis_index("ca")
    z, y = c // NY, c % NY
    zp = lax.rem(c + NY, n)
    zm = lax.rem(c + n - NY, n)
    yp = z * NY + lax.rem(y + 1, NY)
    ym = z * NY + lax.rem(y + NY - 1, NY)
    cp1, cm1 = lax.rem(c + 1, n), lax.rem(c + n - 1, n)
    cp3, cm3 = lax.rem(c + 3, n), lax.rem(c + n - 3, n)

    barrier = pltpu.get_barrier_semaphore()
    for other in (zp, zm, yp, ym, cp1, cm1, cp3, cm3):
        pl.semaphore_signal(barrier, inc=1, device_id={"ca": other}, device_id_type=MESH)

    off = [pl.multiple_of(rows * lax.rem(y + r, NY), rows) for r in range(NY)]

    def local(src, dst, i):
        return pltpu.make_async_copy(src, dst, loc_sem.at[i])

    own = pl.ds(off[0], rows)
    kw = wk_hbm.shape[1]
    cp_k = local(wk_hbm, kvbuf.at[0, own, pl.ds(0, kw)], 0)
    cp_v = local(wv_hbm, kvbuf.at[0, own, pl.ds(kw, kw)], 1)
    cp_q = local(wq_hbm, qbuf.at[0, own], 2)
    cp_x = local(x_hbm, xbuf, 3)
    cp_c = local(cos_hbm, cosb, 4)
    cp_s = local(sin_hbm, sinb, 5)
    for cp in (cp_k, cp_v, cp_q, cp_x, cp_c, cp_s):
        cp.start()

    def remote(src, dst, ssem, rsem, to):
        return pltpu.make_async_remote_copy(
            src_ref=src, dst_ref=dst, send_sem=ssem, recv_sem=rsem,
            device_id={"ca": to}, device_id_type=MESH,
        )

    def qz(s_from, s_to, d):
        return remote(
            qbuf.at[s_from, own], qbuf.at[s_to, own], qz_s.at[s_to], qz_r.at[s_to],
            zp if d == 0 else zm,
        )

    def qy_region(kind, receiver):
        r = {0: 3, 1: 1, 2: 2, 3: 2}[kind] if receiver else {0: 0, 1: 0, 2: 3, 3: 1}[kind]
        if kind < 2:
            return pl.ds(off[r], rows)
        return pl.ds(pl.multiple_of(off[r] + (kind - 2) * hr, hr), hr)

    def qy(kind, s, receiver=False):
        region = qbuf.at[s, qy_region(kind, receiver)]
        return remote(region, region, qy_s.at[kind, s], qy_r.at[kind, s], yp if kind % 2 == 0 else ym)

    def ky(kind, receiver=False):
        region = kvbuf.at[0, qy_region(kind, receiver)]
        return remote(region, region, ky_s.at[kind], ky_r.at[kind], yp if kind % 2 == 0 else ym)

    def kz(s_from, s_to, r, d):
        region = pl.ds(off[r], rows)
        return remote(
            kvbuf.at[s_from, region], kvbuf.at[s_to, region], kz_s.at[s_to, r], kz_r.at[s_to, r],
            zp if d == 0 else zm,
        )

    def columns(s):
        origin = lax.rem(z - s + nz, nz)
        return pl.ds(pl.multiple_of(origin * block, block), block)

    def product(buf, s):
        return jnp.dot(xbuf[:, columns(s)], buf[s], preferred_element_type=jnp.float32)

    pl.semaphore_wait(barrier, 8)

    cp_k.wait()
    cp_v.wait()
    ky(0).start()
    ky(1).start()
    kz(0, 1, 0, 0).start()
    kz(0, nz - 1, 0, 1).start()
    cp_q.wait()
    qz(0, 1, 0).start()
    qz(0, nz - 1, 1).start()
    qy(0, 0).start()
    qy(1, 0).start()
    ky(0, True).wait_recv()
    ky(2).start()
    kz(0, 1, 3, 0).start()
    kz(0, nz - 1, 3, 1).start()
    ky(1, True).wait_recv()
    ky(3).start()
    kz(0, 1, 1, 0).start()
    kz(0, nz - 1, 1, 1).start()
    ky(2, True).wait_recv()
    ky(3, True).wait_recv()
    kz(0, 1, 2, 0).start()
    kz(0, nz - 1, 2, 1).start()
    cp_x.wait()
    acckv[...] = product(kvbuf, 0)
    qy(0, 0, True).wait_recv()
    qy(2, 0).start()
    qy(1, 0, True).wait_recv()
    qy(3, 0).start()

    order = (0, 3, 1, 2)

    def step(d, carry):
        up, down = d, nz - d
        qz(up, up, 0).wait_recv()
        qz(up, up + 1, 0).start()
        qy(0, up).start()
        qy(1, up).start()
        qz(down, down, 1).wait_recv()

        @pl.when(d < half - 1)
        def _():
            qz(down, down - 1, 1).start()

        qy(0, down).start()
        qy(1, down).start()
        for i, r in enumerate(order):
            kz(up, up, r, 0).wait_recv()
            if i < 2:
                kz(up, up + 1, r, 0).start()
            else:
                @pl.when(d < half - 1)
                def _():
                    kz(up, up + 1, r, 0).start()
            kz(down, down, r, 1).wait_recv()
            if i >= 2:
                kz(down, down - 1, r, 1).start()
            else:
                @pl.when(d < half - 1)
                def _():
                    kz(down, down - 1, r, 1).start()
        for s in (up, down):
            qy(0, s, True).wait_recv()
            qy(2, s).start()
            qy(1, s, True).wait_recv()
            qy(3, s).start()
        acckv[...] += product(kvbuf, up) + product(kvbuf, down)

        @pl.when(d == 1)
        def _():
            qy(2, 0, True).wait_recv()
            qy(3, 0, True).wait_recv()
            accq[...] = product(qbuf, 0)

        @pl.when(d > 1)
        def _():
            for s in (up - 1, down + 1):
                qy(2, s, True).wait_recv()
                qy(3, s, True).wait_recv()
            accq[...] += product(qbuf, up - 1) + product(qbuf, down + 1)

        return carry

    lax.fori_loop(1, half, step, 0)

    qz(half, half, 0).wait_recv()
    qy(0, half).start()
    qy(1, half).start()
    for i, r in enumerate(order):
        kz(half, half, r, 0 if i < 2 else 1).wait_recv()
    cp_c.wait()
    cp_s.wait()
    cosine, sine_part = cosb[...], sinb[...]

    def rotated(values):
        return values * cosine + pltpu.roll(values, HEAD_DIM // 2, 1) * sine_part

    total = acckv[...] + product(kvbuf, half)
    win[0, :, 0:HEAD_DIM] = rotated(total[:, :HEAD_DIM]).astype(jnp.bfloat16)
    win[0, :, HEAD_DIM:] = total[:, HEAD_DIM:].astype(jnp.bfloat16)
    qy(0, half, True).wait_recv()
    qy(2, half).start()
    qy(1, half, True).wait_recv()
    qy(3, half).start()

    tok = win.shape[1]
    upper, lower = pl.ds(0, tok // 2), pl.ds(tok // 2, tok // 2)

    def halo(i, src, dst, region, to):
        return remote(win.at[src, region], win.at[dst, region], h_s.at[i], h_r.at[i], to)

    sends = [
        halo(0, 0, 1, upper, cp1),
        halo(1, 0, 3, lower, cp3),
        halo(2, 0, 1, lower, cp1),
        halo(3, 0, 3, upper, cp3),
        halo(4, 1, 2, upper, cp1),
        halo(5, 3, 2, lower, cm1),
    ]
    for i in range(4):
        sends[i].start()
    for s in (half - 1, half + 1):
        qy(2, s, True).wait_recv()
        qy(3, s, True).wait_recv()
    accq[...] += product(qbuf, half - 1) + product(qbuf, half + 1)
    sends[0].wait_recv()
    sends[4].start()
    sends[1].wait_recv()
    sends[5].start()
    qy(2, half, True).wait_recv()
    qy(3, half, True).wait_recv()
    total = accq[...] + product(qbuf, half)
    for h in range(GROUP):
        part = slice(h * HEAD_DIM, (h + 1) * HEAD_DIM)
        q_out[:, part] = rotated(total[:, part]).astype(jnp.bfloat16)

    def put(i):
        return pltpu.make_async_copy(win.at[i], win_out.at[REACH - i], o_sem.at[i])

    put(0).start()
    sends[2].wait_recv()
    put(1).start()
    sends[3].wait_recv()
    put(3).start()
    sends[4].wait_recv()
    sends[5].wait_recv()
    put(2).start()
    for i in range(REACH + 1):
        put(i).wait()

    for copy in sends:
        copy.wait_send()
    for kind in range(4):
        ky(kind).wait_send()

    def drain(s, carry):
        qz(s, s, 0).wait_send()
        for r in range(NY):
            kz(s, s, r, 0).wait_send()
        return carry

    lax.fori_loop(1, nz, drain, 0)

    def drain_y(s, carry):
        for kind in range(4):
            qy(kind, s).wait_send()
        return carry

    lax.fori_loop(0, nz, drain_y, 0)


def attention_kernel(first_ref, q_ref, win_ref, start_ref, out_ref, vext, acc):
    keys = win_ref.shape[0]
    tok = q_ref.shape[0]
    margin = keys - tok
    scale = 1.0 / (math.sqrt(HEAD_DIM) * logit_cap)
    gain = logit_cap * math.log2(math.e)
    vext[:, :HEAD_DIM] = win_ref[:, HEAD_DIM:]
    vext[:, HEAD_DIM:] = jnp.ones((keys, HEAD_DIM), jnp.bfloat16)

    def tile(t, carry):
        rows = pl.ds(pl.multiple_of(t * TILE, TILE), TILE)
        q4 = jnp.concatenate(
            [q_ref[rows, h * HEAD_DIM:(h + 1) * HEAD_DIM] for h in range(GROUP)], axis=0
        )
        acc[...] = jnp.zeros_like(acc)
        start = start_ref[rows, :]
        start = jnp.concatenate([start, start], axis=1)
        row = margin + t * TILE + lax.broadcasted_iota(jnp.int32, (TILE, KEY_BLOCK), 0)
        col = lax.broadcasted_iota(jnp.int32, (TILE, KEY_BLOCK), 1)

        def block(b, carry):
            at = pl.ds(pl.multiple_of(b * KEY_BLOCK, KEY_BLOCK), KEY_BLOCK)
            key = win_ref[at, :HEAD_DIM]
            raw = lax.dot_general(
                q4, key, (((1,), (1,)), ((), ())), preferred_element_type=jnp.float32
            )
            weight = jnp.exp2(gain * jnp.tanh(raw * scale))
            k_id = col + b * KEY_BLOCK
            allowed = (k_id <= row) & (k_id >= start)
            weight = jnp.where(
                jnp.concatenate([allowed] * GROUP, axis=0), weight, 0.0
            ).astype(jnp.bfloat16)
            acc[...] += jnp.dot(weight, vext[at, :], preferred_element_type=jnp.float32)
            return carry

        last = (margin + t * TILE + TILE - 1) // KEY_BLOCK
        lax.fori_loop(first_ref[t], last + 1, block, 0)
        mixed = acc[:, :HEAD_DIM] / acc[:, HEAD_DIM:]
        for h in range(GROUP):
            out_ref[rows, h * HEAD_DIM:(h + 1) * HEAD_DIM] = (
                mixed[h * TILE:(h + 1) * TILE].astype(jnp.bfloat16)
            )
        return carry

    lax.fori_loop(0, tok // TILE, tile, 0)


def per_device(tokens, lengths, w_query, w_key, w_value):
    tok, depth = tokens.shape
    rows, q_width = w_query.shape
    kv_width = w_key.shape[1] + w_value.shape[1]
    nz = lax.axis_size("ca") // NY
    block = rows * NY
    c = lax.axis_index("ca")
    row_ids = c * tok + jnp.arange(tok, dtype=jnp.int32)
    starts = doc_starts(lengths, row_ids)
    half_dim = HEAD_DIM // 2
    frequency = rope_theta ** (-(jnp.arange(half_dim, dtype=jnp.float32) * 2.0) / HEAD_DIM)
    angles = (row_ids - starts).astype(jnp.float32)[:, None] * frequency[None, :]
    cosine, sine_part = jnp.cos(angles), jnp.sin(angles)
    cosine = jnp.concatenate([cosine, cosine], axis=1)
    sine_part = jnp.concatenate([-sine_part, sine_part], axis=1)

    any_spec = pl.BlockSpec(memory_space=pl.ANY)
    vmem_spec = pl.BlockSpec(memory_space=pltpu.VMEM)
    dma = pltpu.SemaphoreType.DMA
    query, window = pl.pallas_call(
        functools.partial(gather_kernel, nz),
        out_shape=(
            jax.ShapeDtypeStruct((tok, q_width), jnp.bfloat16),
            jax.ShapeDtypeStruct((REACH + 1, tok, kv_width), jnp.bfloat16),
        ),
        in_specs=[any_spec] * 6,
        out_specs=(vmem_spec, any_spec),
        scratch_shapes=[
            pltpu.VMEM((tok, depth), jnp.bfloat16),
            pltpu.VMEM((nz, block, q_width), jnp.bfloat16),
            pltpu.VMEM((nz, block, kv_width), jnp.bfloat16),
            pltpu.VMEM((tok, q_width), jnp.float32),
            pltpu.VMEM((tok, kv_width), jnp.float32),
            pltpu.VMEM((tok, HEAD_DIM), jnp.float32),
            pltpu.VMEM((tok, HEAD_DIM), jnp.float32),
            pltpu.VMEM((REACH + 1, tok, kv_width), jnp.bfloat16),
            dma((6,)),
            dma((nz,)), dma((nz,)),
            dma((4, nz)), dma((4, nz)),
            dma((nz, NY)), dma((nz, NY)),
            dma((4,)), dma((4,)),
            dma((6,)), dma((6,)),
            dma((REACH + 1,)),
        ],
        compiler_params=pltpu.CompilerParams(collective_id=0, has_side_effects=True),
        name="gather_project",
    )(tokens, w_query, w_key, w_value, cosine, sine_part)

    base = (c - REACH) * tok
    local_start = starts - base
    first = local_start[::TILE] // KEY_BLOCK
    return pl.pallas_call(
        attention_kernel,
        out_shape=jax.ShapeDtypeStruct((tok, q_width), jnp.bfloat16),
        in_specs=[pl.BlockSpec(memory_space=pltpu.SMEM), vmem_spec, vmem_spec, vmem_spec],
        out_specs=vmem_spec,
        scratch_shapes=[
            pltpu.VMEM(((REACH + 1) * tok, 2 * HEAD_DIM), jnp.bfloat16),
            pltpu.VMEM((GROUP * TILE, 2 * HEAD_DIM), jnp.float32),
        ],
        name="attention",
    )(
        first,
        query,
        window.reshape((REACH + 1) * tok, kv_width),
        jnp.broadcast_to(local_start[:, None], (tok, HEAD_DIM)),
    )


def solution(mesh):
    placed = (P("ca", None), P(), P("ca", "tp"), P("ca", "tp"), P("ca", "tp"))
    return jax.shard_map(
        per_device, mesh=mesh, in_specs=placed, out_specs=P("ca", "tp"), check_vma=False
    )
```

```python
import functools
import math

import jax
import jax.numpy as jnp
import numpy as np
from jax import lax
from jax.experimental import pallas as pl
from jax.experimental.pallas import tpu as pltpu
from jax.sharding import PartitionSpec as P

GROUP = 4
HEAD_DIM = 128
REACH = 3
NY = 4
LAG = 3

rope_theta = 500000.0
logit_cap = 5.0

MESH = pl.DeviceIdType.MESH


def gather_kernel(
    nz,
    len_ref, freq_ref, x_hbm, wq_hbm, wk_hbm, wv_hbm,
    out_ref,
    xbuf, qbuf, kvbuf, accq, acckv, cosb, sinb, startb, win, query, acc,
    loc_sem, qz_s, qz_r, qy_s, qy_r, qh_s, qh_r, kz_s, kz_r, ky_s, ky_r, h_s, h_r,
):
    n = nz * NY
    half = nz // 2
    rows = wq_hbm.shape[0]
    block = rows * NY
    hr = rows // 2
    c = lax.axis_index("ca")
    z, y = c // NY, c % NY
    zp = lax.rem(c + NY, n)
    zm = lax.rem(c + n - NY, n)
    yp = z * NY + lax.rem(y + 1, NY)
    ym = z * NY + lax.rem(y + NY - 1, NY)
    y2 = z * NY + lax.rem(y + 2, NY)
    later = [lax.rem(c + i + 1, n) for i in range(REACH)]
    earlier = [lax.rem(c + n - i - 1, n) for i in range(REACH)]
    partners = [zp, zm, yp, ym, y2] + later + earlier

    barrier = pltpu.get_barrier_semaphore()
    for other in partners:
        pl.semaphore_signal(barrier, inc=1, device_id={"ca": other}, device_id_type=MESH)

    off = [pl.multiple_of(rows * lax.rem(y + r, NY), rows) for r in range(NY)]

    def local(src, dst, i):
        return pltpu.make_async_copy(src, dst, loc_sem.at[i])

    own = pl.ds(off[0], rows)
    kw = wk_hbm.shape[1]
    cp_k = local(wk_hbm, kvbuf.at[0, own, pl.ds(0, kw)], 0)
    cp_v = local(wv_hbm, kvbuf.at[0, own, pl.ds(kw, kw)], 1)
    cp_q = local(wq_hbm, qbuf.at[0, own], 2)
    cp_x = local(x_hbm, xbuf, 3)
    for cp in (cp_k, cp_v, cp_q, cp_x):
        cp.start()

    def remote(src, dst, ssem, rsem, to):
        return pltpu.make_async_remote_copy(
            src_ref=src, dst_ref=dst, send_sem=ssem, recv_sem=rsem,
            device_id={"ca": to}, device_id_type=MESH,
        )

    def qz(s_from, s_to, d):
        return remote(
            qbuf.at[s_from, own], qbuf.at[s_to, own], qz_s.at[s_to], qz_r.at[s_to],
            zp if d == 0 else zm,
        )

    y_to = (yp, ym, y2)
    y_off = (3, 1, 2)

    def qy(kind, s, receiver=False):
        region = qbuf.at[s, pl.ds(off[y_off[kind] if receiver else 0], rows)]
        return remote(region, region, qy_s.at[kind, s], qy_r.at[kind, s], y_to[kind])

    def qh(kind, s, receiver=False):
        at = off[2] if receiver else off[y_off[kind]]
        region = qbuf.at[s, pl.ds(pl.multiple_of(at + kind * hr, hr), hr)]
        return remote(region, region, qh_s.at[kind, s], qh_r.at[kind, s], y_to[kind])

    def q_pass(s):
        for kind in range(2):
            qy(kind, s, True).wait_recv()
            qh(kind, s).start()

    def ky(kind, receiver=False):
        region = kvbuf.at[0, pl.ds(off[y_off[kind] if receiver else 0], rows)]
        return remote(region, region, ky_s.at[kind], ky_r.at[kind], y_to[kind])

    def kz(s_from, s_to, r, d):
        region = pl.ds(off[r], rows)
        return remote(
            kvbuf.at[s_from, region], kvbuf.at[s_to, region], kz_s.at[s_to, r], kz_r.at[s_to, r],
            zp if d == 0 else zm,
        )

    def columns(s):
        origin = lax.rem(z - s + nz, nz)
        return pl.ds(pl.multiple_of(origin * block, block), block)

    def product(buf, s):
        return jnp.dot(xbuf[:, columns(s)], buf[s], preferred_element_type=jnp.float32)

    def kz_pass(d, r, up_more, down_more):
        kz(d, d, r, 0).wait_recv()
        up_more(lambda: kz(d, d + 1, r, 0).start())
        kz(nz - d, nz - d, r, 1).wait_recv()
        down_more(lambda: kz(nz - d, nz - d - 1, r, 1).start())

    def q_ready(s):
        for kind in range(2):
            qh(kind, s, True).wait_recv()

    tok = x_hbm.shape[0]
    chunk = tok // half

    def prepare(i):
        at = pl.ds(pl.multiple_of(i * chunk, chunk), chunk)
        row = c * tok + i * chunk + lax.broadcasted_iota(jnp.int32, (chunk, HEAD_DIM), 0)
        start = jnp.zeros_like(row)
        end = jnp.int32(0)
        for doc in range(len_ref.shape[0]):
            end = end + len_ref[doc]
            start = jnp.where(row >= end, end, start)
        angle = (row - start).astype(jnp.float32) * freq_ref[0:1, :]
        lane = lax.broadcasted_iota(jnp.int32, (chunk, HEAD_DIM), 1)
        sine = jnp.sin(angle)
        cosb[at, :] = jnp.cos(angle)
        sinb[at, :] = jnp.where(lane < HEAD_DIM // 2, -sine, sine)
        startb[at, :] = start - (c - REACH) * tok

    pl.semaphore_wait(barrier, len(partners))

    cp_k.wait()
    cp_v.wait()
    for kind in range(3):
        ky(kind).start()
    kz(0, 1, 0, 0).start()
    kz(0, nz - 1, 0, 1).start()
    cp_q.wait()
    qz(0, 1, 0).start()
    qz(0, nz - 1, 1).start()
    for kind in range(2):
        qy(kind, 0).start()
    prepare(0)
    for kind in range(3):
        ky(kind, True).wait_recv()
        kz(0, 1, y_off[kind], 0).start()
        kz(0, nz - 1, y_off[kind], 1).start()
    cp_x.wait()
    acckv[...] = product(kvbuf, 0)

    def step(d, carry):
        up, down = d, nz - d
        always = lambda f: f()
        inner = pl.when(d < half - 1)

        kz_pass(d, 0, always, inner)
        qz(up, up, 0).wait_recv()
        qz(up, up + 1, 0).start()
        qz(down, down, 1).wait_recv()

        @inner
        def _():
            qz(down, down - 1, 1).start()

        for kind in range(2):
            qy(kind, up).start()
        for kind in range(2):
            qy(kind, down).start()

        @pl.when(d > 1)
        def _():
            acckv[...] += product(kvbuf, up - 1) + product(kvbuf, down + 1)

        kz_pass(d, 3, always, inner)
        prepare(d)

        @pl.when(d == 2)
        def _():
            q_pass(0)

        @pl.when(d > 2)
        def _():
            q_pass(up - 2)

        @pl.when(d == LAG)
        def _():
            q_ready(0)
            accq[...] = product(qbuf, 0)

        @pl.when(d > LAG)
        def _():
            q_ready(up - LAG)
            accq[...] += product(qbuf, up - LAG)

        kz_pass(d, 1, inner, always)

        @pl.when(d > 2)
        def _():
            q_pass(down + 2)

        @pl.when(d > LAG)
        def _():
            q_ready(down + LAG)
            accq[...] += product(qbuf, down + LAG)

        kz_pass(d, 2, inner, always)
        return carry

    lax.fori_loop(1, half, step, 0)

    kz(half, half, 0, 0).wait_recv()
    qz(half, half, 0).wait_recv()
    for kind in range(3):
        qy(kind, half).start()
    q_pass(half - 2)
    q_pass(half + 2)
    acckv[...] += product(kvbuf, half - 1) + product(kvbuf, half + 1)
    cosine, sine_part = cosb[...], sinb[...]

    def rotated(values):
        return values * cosine + pltpu.roll(values, HEAD_DIM // 2, 1) * sine_part

    kz(half, half, 3, 0).wait_recv()
    kz(half, half, 1, 1).wait_recv()
    kz(half, half, 2, 1).wait_recv()
    q_pass(half - 1)
    q_pass(half + 1)
    total = acckv[...] + product(kvbuf, half)
    win[0, :, 0:HEAD_DIM] = rotated(total[:, :HEAD_DIM]).astype(jnp.bfloat16)
    win[0, :, HEAD_DIM:] = total[:, HEAD_DIM:].astype(jnp.bfloat16)

    def halo(i):
        to = later[i] if isinstance(i, int) else later[0]
        return remote(win.at[0], win.at[i + 1], h_s.at[i], h_r.at[i], to)

    for i in range(REACH):
        halo(i).start()
    for d in range(half - LAG, half):
        q_ready(d)
        q_ready(nz - d)
        accq[...] += product(qbuf, d) + product(qbuf, nz - d)
    for kind in range(3):
        qy(kind, half, True).wait_recv()
    total = accq[...] + product(qbuf, half)
    for h in range(GROUP):
        part = slice(h * HEAD_DIM, (h + 1) * HEAD_DIM)
        query[:, part] = rotated(total[:, part]).astype(jnp.bfloat16)

    scale = 1.0 / (math.sqrt(HEAD_DIM) * logit_cap)
    gain = logit_cap * math.log2(math.e)

    def attend(r0, r_num, block, k0, k_num, own_keys=False):
        r, k = slice(r0, r0 + r_num), slice(k0, k0 + k_num)
        key = win[block, k, :HEAD_DIM]
        value = jnp.concatenate(
            [win[block, k, HEAD_DIM:], jnp.ones((k_num, HEAD_DIM), jnp.bfloat16)], axis=1
        )
        col = lax.broadcasted_iota(jnp.int32, (r_num, k_num), 1) + (REACH - block) * tok + k0
        start = startb[r, :]
        allowed = col >= jnp.concatenate([start] * (k_num // HEAD_DIM), axis=1)
        if own_keys:
            row = lax.broadcasted_iota(jnp.int32, (r_num, k_num), 0) + REACH * tok + r0
            allowed = allowed & (col <= row)
        for h in range(GROUP):
            raw = lax.dot_general(
                query[r, h * HEAD_DIM:(h + 1) * HEAD_DIM], key,
                (((1,), (1,)), ((), ())), preferred_element_type=jnp.float32,
            )
            weight = jnp.exp2(gain * jnp.tanh(raw * scale))
            weight = jnp.where(allowed, weight, 0.0).astype(jnp.bfloat16)
            part = jnp.dot(weight, value, preferred_element_type=jnp.float32)
            if own_keys:
                acc[h, r, :] = part
            else:
                acc[h, r, :] += part

    mid = tok // 2
    attend(0, mid, 0, 0, mid, True)
    attend(mid, mid, 0, 0, tok, True)

    def nearer(block, carry):
        halo(block - 1).wait_recv()
        attend(0, tok, block, 0, tok)
        return carry

    lax.fori_loop(1, REACH, nearer, 0)
    halo(REACH - 1).wait_recv()
    attend(0, mid, REACH, 0, tok)
    attend(mid, mid, REACH, mid, mid)
    for h in range(GROUP):
        out_ref[:, h * HEAD_DIM:(h + 1) * HEAD_DIM] = (
            acc[h, :, :HEAD_DIM] / acc[h, :, HEAD_DIM:]
        ).astype(jnp.bfloat16)

    for i in range(REACH):
        halo(i).wait_send()
    for kind in range(3):
        ky(kind).wait_send()

    def drain(s, carry):
        qz(s, s, 0).wait_send()
        for r in range(NY):
            kz(s, s, r, 0).wait_send()
        return carry

    lax.fori_loop(1, nz, drain, 0)

    def drain_y(s, carry):
        for kind in range(2):
            qy(kind, s).wait_send()

            @pl.when(s != half)
            def _():
                qh(kind, s).wait_send()

        return carry

    lax.fori_loop(0, nz, drain_y, 0)
    qy(2, half).wait_send()


def per_device(tokens, lengths, w_query, w_key, w_value):
    tok, depth = tokens.shape
    rows, q_width = w_query.shape
    kv_width = w_key.shape[1] + w_value.shape[1]
    nz = lax.axis_size("ca") // NY
    block = rows * NY
    half_dim = HEAD_DIM // 2
    frequency = rope_theta ** (-(np.arange(half_dim, dtype=np.float32) * 2.0) / HEAD_DIM)
    frequency = np.tile(np.concatenate([frequency, frequency]).astype(np.float32), (8, 1))

    any_spec = pl.BlockSpec(memory_space=pl.ANY)
    vmem_spec = pl.BlockSpec(memory_space=pltpu.VMEM)
    dma = pltpu.SemaphoreType.DMA
    return pl.pallas_call(
        functools.partial(gather_kernel, nz),
        out_shape=jax.ShapeDtypeStruct((tok, q_width), jnp.bfloat16),
        in_specs=[pl.BlockSpec(memory_space=pltpu.SMEM), vmem_spec] + [any_spec] * 4,
        out_specs=vmem_spec,
        scratch_shapes=[
            pltpu.VMEM((tok, depth), jnp.bfloat16),
            pltpu.VMEM((nz, block, q_width), jnp.bfloat16),
            pltpu.VMEM((nz, block, kv_width), jnp.bfloat16),
            pltpu.VMEM((tok, q_width), jnp.float32),
            pltpu.VMEM((tok, kv_width), jnp.float32),
            pltpu.VMEM((tok, HEAD_DIM), jnp.float32),
            pltpu.VMEM((tok, HEAD_DIM), jnp.float32),
            pltpu.VMEM((tok, HEAD_DIM), jnp.int32),
            pltpu.VMEM((REACH + 1, tok, kv_width), jnp.bfloat16),
            pltpu.VMEM((tok, q_width), jnp.bfloat16),
            pltpu.VMEM((GROUP, tok, 2 * HEAD_DIM), jnp.float32),
            dma((4,)),
            dma((nz,)), dma((nz,)),
            dma((3, nz)), dma((3, nz)),
            dma((2, nz)), dma((2, nz)),
            dma((nz, NY)), dma((nz, NY)),
            dma((3,)), dma((3,)),
            dma((REACH,)), dma((REACH,)),
        ],
        compiler_params=pltpu.CompilerParams(collective_id=0, has_side_effects=True),
        name="gather_project",
    )(lengths, jnp.asarray(frequency), tokens, w_query, w_key, w_value)


def solution(mesh):
    placed = (P("ca", None), P(), P("ca", "tp"), P("ca", "tp"), P("ca", "tp"))
    return jax.shard_map(
        per_device, mesh=mesh, in_specs=placed, out_specs=P("ca", "tp"), check_vma=False
    )
```

```python
import functools
import math

import jax
import jax.numpy as jnp
import numpy as np
from jax import lax
from jax.experimental import pallas as pl
from jax.experimental.pallas import tpu as pltpu
from jax.sharding import PartitionSpec as P

GROUP = 4
HEAD_DIM = 128
REACH = 3
NY = 4
LAG = 3

rope_theta = 500000.0
logit_cap = 5.0

MESH = pl.DeviceIdType.MESH


def gather_kernel(
    nz,
    len_hbm, freq_hbm, x_hbm, wq_hbm, wk_hbm, wv_hbm,
    out_ref,
    xbuf, qbuf, kvbuf, accq, acckv, cosb, sinb, startb, win, query, acc, len_ref, freq_ref,
    loc_sem, qz_s, qz_r, qy_s, qy_r, qh_s, qh_r, kz_s, kz_r, ky_s, ky_r, h_s, h_r, qp_s, qp_r,
):
    n = nz * NY
    half = nz // 2
    rows = wq_hbm.shape[0]
    block = rows * NY
    hr = rows // 2
    c = lax.axis_index("ca")
    z, y = c // NY, c % NY
    zp = lax.rem(c + NY, n)
    zm = lax.rem(c + n - NY, n)
    yp = z * NY + lax.rem(y + 1, NY)
    ym = z * NY + lax.rem(y + NY - 1, NY)
    y2 = z * NY + lax.rem(y + 2, NY)
    cp1, cm1 = lax.rem(c + 1, n), lax.rem(c + n - 1, n)
    cp3, cm3 = lax.rem(c + REACH, n), lax.rem(c + n - REACH, n)
    partners = [zp, zm, yp, ym, y2, cp1, cm1, cp3, cm3]

    barrier = pltpu.get_barrier_semaphore()
    for other in partners:
        pl.semaphore_signal(barrier, inc=1, device_id={"ca": other}, device_id_type=MESH)

    off = [pl.multiple_of(rows * lax.rem(y + r, NY), rows) for r in range(NY)]

    def local(src, dst, i):
        return pltpu.make_async_copy(src, dst, loc_sem.at[i])

    own = pl.ds(off[0], rows)
    kw = wk_hbm.shape[1]
    cp_k = local(wk_hbm, kvbuf.at[0, own, pl.ds(0, kw)], 0)
    cp_v = local(wv_hbm, kvbuf.at[0, own, pl.ds(kw, kw)], 1)
    cp_q = local(wq_hbm, qbuf.at[0, own], 2)
    cp_x = local(x_hbm, xbuf, 3)
    cp_l = local(len_hbm, len_ref, 4)
    cp_f = local(freq_hbm, freq_ref, 5)
    for cp in (cp_k, cp_v, cp_q, cp_l, cp_f, cp_x):
        cp.start()

    def remote(src, dst, ssem, rsem, to):
        return pltpu.make_async_remote_copy(
            src_ref=src, dst_ref=dst, send_sem=ssem, recv_sem=rsem,
            device_id={"ca": to}, device_id_type=MESH,
        )

    def qz(s_from, s_to, d):
        return remote(
            qbuf.at[s_from, own], qbuf.at[s_to, own], qz_s.at[s_to], qz_r.at[s_to],
            zp if d == 0 else zm,
        )

    y_to = (yp, ym, y2)
    y_off = (3, 1, 2)

    def qy(kind, s, receiver=False):
        region = qbuf.at[s, pl.ds(off[y_off[kind] if receiver else 0], rows)]
        return remote(region, region, qy_s.at[kind, s], qy_r.at[kind, s], y_to[kind])

    def qh(kind, s, receiver=False):
        at = off[2] if receiver else off[y_off[kind]]
        region = qbuf.at[s, pl.ds(pl.multiple_of(at + kind * hr, hr), hr)]
        return remote(region, region, qh_s.at[kind, s], qh_r.at[kind, s], y_to[kind])

    def q_pass(s, further=lambda r: None):
        for kind in range(2):
            qy(kind, s, True).wait_recv()
            qh(kind, s).start()
            further(y_off[kind])

    def qp(s_from, s_to, r):
        region = pl.ds(off[r], rows)
        i = s_to - (half - 1)
        return remote(
            qbuf.at[s_from, region], qbuf.at[s_to, region], qp_s.at[i, r], qp_r.at[i, r],
            zp if s_to > s_from else zm,
        )

    def ky(kind, receiver=False):
        region = kvbuf.at[0, pl.ds(off[y_off[kind] if receiver else 0], rows)]
        return remote(region, region, ky_s.at[kind], ky_r.at[kind], y_to[kind])

    def kz(s_from, s_to, r, d):
        region = pl.ds(off[r], rows)
        return remote(
            kvbuf.at[s_from, region], kvbuf.at[s_to, region], kz_s.at[s_to, r], kz_r.at[s_to, r],
            zp if d == 0 else zm,
        )

    def columns(s):
        origin = lax.rem(z - s + nz, nz)
        return pl.ds(pl.multiple_of(origin * block, block), block)

    def product(buf, s):
        return jnp.dot(xbuf[:, columns(s)], buf[s], preferred_element_type=jnp.float32)

    def kz_pass(d, r, up_more, down_more):
        kz(d, d, r, 0).wait_recv()
        up_more(lambda: kz(d, d + 1, r, 0).start())
        kz(nz - d, nz - d, r, 1).wait_recv()
        down_more(lambda: kz(nz - d, nz - d - 1, r, 1).start())

    def q_ready(s):
        for kind in range(2):
            qh(kind, s, True).wait_recv()

    tok = x_hbm.shape[0]
    chunk = tok // half

    def prepare(i):
        at = pl.ds(pl.multiple_of(i * chunk, chunk), chunk)
        row = c * tok + i * chunk + lax.broadcasted_iota(jnp.int32, (chunk, HEAD_DIM), 0)
        start = jnp.zeros_like(row)
        end = jnp.int32(0)
        for doc in range(len_ref.shape[0]):
            end = end + len_ref[doc]
            start = jnp.where(row >= end, end, start)
        angle = (row - start).astype(jnp.float32) * freq_ref[0:1, :]
        lane = lax.broadcasted_iota(jnp.int32, (chunk, HEAD_DIM), 1)
        sine = jnp.sin(angle)
        cosb[at, :] = jnp.cos(angle)
        sinb[at, :] = jnp.where(lane < HEAD_DIM // 2, -sine, sine)
        startb[at, :] = start - (c - REACH) * tok

    pl.semaphore_wait(barrier, len(partners))

    cp_k.wait()
    cp_v.wait()
    for kind in range(3):
        ky(kind).start()
    kz(0, 1, 0, 0).start()
    kz(0, nz - 1, 0, 1).start()
    cp_q.wait()
    qz(0, 1, 0).start()
    qz(0, nz - 1, 1).start()
    for kind in range(2):
        qy(kind, 0).start()
    cp_l.wait()
    cp_f.wait()
    prepare(0)
    for kind in range(3):
        ky(kind, True).wait_recv()
        kz(0, 1, y_off[kind], 0).start()
        kz(0, nz - 1, y_off[kind], 1).start()
    cp_x.wait()
    acckv[...] = product(kvbuf, 0)

    def step(d, carry):
        up, down = d, nz - d
        always = lambda f: f()
        inner = pl.when(d < half - 1)

        kz_pass(d, 0, always, inner)
        qz(up, up, 0).wait_recv()
        qz(up, up + 1, 0).start()
        qz(down, down, 1).wait_recv()

        @inner
        def _():
            qz(down, down - 1, 1).start()

        @inner
        def _():
            for s in (up, down):
                for kind in range(2):
                    qy(kind, s).start()

        @pl.when(d > 1)
        def _():
            acckv[...] += product(kvbuf, up - 1) + product(kvbuf, down + 1)

        kz_pass(d, 3, always, inner)
        prepare(d)

        @pl.when(d == 2)
        def _():
            q_pass(0)

        @pl.when(d > 2)
        def _():
            q_pass(up - 2)

        @pl.when(d == LAG)
        def _():
            q_ready(0)
            accq[...] = product(qbuf, 0)

        @pl.when(d > LAG)
        def _():
            q_ready(up - LAG)
            accq[...] += product(qbuf, up - LAG)

        kz_pass(d, 1, inner, always)

        @pl.when(d > 2)
        def _():
            q_pass(down + 2)

        @pl.when(d > LAG)
        def _():
            q_ready(down + LAG)
            accq[...] += product(qbuf, down + LAG)

        kz_pass(d, 2, inner, always)
        return carry

    lax.fori_loop(1, half, step, 0)

    q_pass(half - 2, lambda r: qp(half - 2, half - 1, r).start())
    q_pass(half + 2, lambda r: qp(half + 2, half + 1, r).start())
    kz(half, half, 0, 0).wait_recv()
    acckv[...] += product(kvbuf, half - 1) + product(kvbuf, half + 1)
    cosine, sine_part = cosb[...], sinb[...]

    def rotated(values):
        return values * cosine + pltpu.roll(values, HEAD_DIM // 2, 1) * sine_part

    kz(half, half, 3, 0).wait_recv()
    kz(half, half, 1, 1).wait_recv()
    kz(half, half, 2, 1).wait_recv()
    total = acckv[...] + product(kvbuf, half)
    win[0, :, 0:HEAD_DIM] = rotated(total[:, :HEAD_DIM]).astype(jnp.bfloat16)
    win[0, :, HEAD_DIM:] = total[:, HEAD_DIM:].astype(jnp.bfloat16)

    upper, lower = pl.ds(0, tok // 2), pl.ds(tok // 2, tok // 2)

    def halo(i):
        src, dst, region, to = (
            (0, 1, upper, cp1), (0, 3, lower, cp3), (0, 1, lower, cp1), (0, 3, upper, cp3),
            (1, 2, upper, cp1), (3, 2, lower, cm1),
        )[i]
        return remote(win.at[src, region], win.at[dst, region], h_s.at[i], h_r.at[i], to)

    for i in range(4):
        halo(i).start()
    q_ready(half - 2)
    qp(half - 2, half - 1, 2).start()
    q_ready(half + 2)
    qp(half + 2, half + 1, 2).start()
    qp(half - 2, half - 1, 3).wait_recv()
    qp(half - 1, half, 3).start()
    qp(half + 2, half + 1, 1).wait_recv()
    qp(half + 1, half, 1).start()
    for d in range(half - LAG, half - 1):
        if d < half - 2:
            q_ready(d)
            q_ready(nz - d)
        accq[...] += product(qbuf, d) + product(qbuf, nz - d)
    halo(0).wait_recv()
    halo(4).start()
    halo(1).wait_recv()
    halo(5).start()
    qp(half + 2, half + 1, 2).wait_recv()
    qp(half + 1, half, 2).start()
    qp(half + 2, half + 1, 3).wait_recv()
    qp(half - 2, half - 1, 1).wait_recv()
    qp(half - 2, half - 1, 2).wait_recv()
    accq[...] += product(qbuf, half - 1) + product(qbuf, half + 1)
    qz(half, half, 0).wait_recv()
    qp(half - 1, half, 3).wait_recv()
    qp(half + 1, half, 1).wait_recv()
    qp(half + 1, half, 2).wait_recv()
    total = accq[...] + product(qbuf, half)
    for h in range(GROUP):
        part = slice(h * HEAD_DIM, (h + 1) * HEAD_DIM)
        query[:, part] = rotated(total[:, part]).astype(jnp.bfloat16)

    scale = 1.0 / (math.sqrt(HEAD_DIM) * logit_cap)
    gain = logit_cap * math.log2(math.e)

    def attend(r0, r_num, block, k0, k_num, own_keys=False):
        r, k = slice(r0, r0 + r_num), slice(k0, k0 + k_num)
        key = win[block, k, :HEAD_DIM]
        value = jnp.concatenate(
            [win[block, k, HEAD_DIM:], jnp.ones((k_num, HEAD_DIM), jnp.bfloat16)], axis=1
        )
        col = lax.broadcasted_iota(jnp.int32, (r_num, k_num), 1) + (REACH - block) * tok + k0
        start = startb[r, :]
        allowed = col >= jnp.concatenate([start] * (k_num // HEAD_DIM), axis=1)
        if own_keys:
            row = lax.broadcasted_iota(jnp.int32, (r_num, k_num), 0) + REACH * tok + r0
            allowed = allowed & (col <= row)
        for h in range(GROUP):
            raw = lax.dot_general(
                query[r, h * HEAD_DIM:(h + 1) * HEAD_DIM], key,
                (((1,), (1,)), ((), ())), preferred_element_type=jnp.float32,
            )
            weight = jnp.exp2(gain * jnp.tanh(raw * scale))
            weight = jnp.where(allowed, weight, 0.0).astype(jnp.bfloat16)
            part = jnp.dot(weight, value, preferred_element_type=jnp.float32)
            if own_keys:
                acc[h, r, :] = part
            else:
                acc[h, r, :] += part

    mid = tok // 2
    attend(0, mid, 0, 0, mid, True)
    attend(mid, mid, 0, 0, tok, True)

    halo(2).wait_recv()
    attend(0, tok, 1, 0, tok)
    halo(3).wait_recv()
    attend(0, mid, REACH, 0, tok)
    attend(mid, mid, REACH, mid, mid)
    halo(4).wait_recv()
    halo(5).wait_recv()
    attend(0, tok, 2, 0, tok)
    for h in range(GROUP):
        out_ref[:, h * HEAD_DIM:(h + 1) * HEAD_DIM] = (
            acc[h, :, :HEAD_DIM] / acc[h, :, HEAD_DIM:]
        ).astype(jnp.bfloat16)

    for i in range(6):
        halo(i).wait_send()
    for kind in range(3):
        ky(kind).wait_send()
    for s_from, s_to, pieces in (
        (half - 2, half - 1, (1, 2, 3)), (half + 2, half + 1, (1, 2, 3)),
        (half - 1, half, (3,)), (half + 1, half, (1, 2)),
    ):
        for r in pieces:
            qp(s_from, s_to, r).wait_send()

    def drain(s, carry):
        qz(s, s, 0).wait_send()
        for r in range(NY):
            kz(s, s, r, 0).wait_send()
        return carry

    lax.fori_loop(1, nz, drain, 0)

    def drain_y(s, carry):
        @pl.when((s < half - 1) | (s > half + 1))
        def _():
            for kind in range(2):
                qy(kind, s).wait_send()
                qh(kind, s).wait_send()

        return carry

    lax.fori_loop(0, nz, drain_y, 0)


def per_device(tokens, lengths, w_query, w_key, w_value):
    tok, depth = tokens.shape
    rows, q_width = w_query.shape
    kv_width = w_key.shape[1] + w_value.shape[1]
    nz = lax.axis_size("ca") // NY
    block = rows * NY
    half_dim = HEAD_DIM // 2
    frequency = rope_theta ** (-(np.arange(half_dim, dtype=np.float32) * 2.0) / HEAD_DIM)
    frequency = np.tile(np.concatenate([frequency, frequency]).astype(np.float32), (8, 1))

    hbm_spec = pl.BlockSpec(memory_space=pltpu.MemorySpace.HBM)
    vmem_spec = pl.BlockSpec(memory_space=pltpu.VMEM)
    dma = pltpu.SemaphoreType.DMA
    return pl.pallas_call(
        functools.partial(gather_kernel, nz),
        out_shape=jax.ShapeDtypeStruct((tok, q_width), jnp.bfloat16),
        in_specs=[hbm_spec] * 6,
        out_specs=vmem_spec,
        scratch_shapes=[
            pltpu.VMEM((tok, depth), jnp.bfloat16),
            pltpu.VMEM((nz, block, q_width), jnp.bfloat16),
            pltpu.VMEM((nz, block, kv_width), jnp.bfloat16),
            pltpu.VMEM((tok, q_width), jnp.float32),
            pltpu.VMEM((tok, kv_width), jnp.float32),
            pltpu.VMEM((tok, HEAD_DIM), jnp.float32),
            pltpu.VMEM((tok, HEAD_DIM), jnp.float32),
            pltpu.VMEM((tok, HEAD_DIM), jnp.int32),
            pltpu.VMEM((REACH + 1, tok, kv_width), jnp.bfloat16),
            pltpu.VMEM((tok, q_width), jnp.bfloat16),
            pltpu.VMEM((GROUP, tok, 2 * HEAD_DIM), jnp.float32),
            pltpu.SMEM(lengths.shape, jnp.int32),
            pltpu.VMEM(frequency.shape, jnp.float32),
            dma((6,)),
            dma((nz,)), dma((nz,)),
            dma((2, nz)), dma((2, nz)),
            dma((2, nz)), dma((2, nz)),
            dma((nz, NY)), dma((nz, NY)),
            dma((3,)), dma((3,)),
            dma((6,)), dma((6,)),
            dma((3, NY)), dma((3, NY)),
        ],
        compiler_params=pltpu.CompilerParams(
            collective_id=0, has_side_effects=True
        ),
        name="gather_project",
    )(lengths, jnp.asarray(frequency), tokens, w_query, w_key, w_value)


def solution(mesh):
    placed = (P("ca", None), P(), P("ca", "tp"), P("ca", "tp"), P("ca", "tp"))
    return jax.shard_map(
        per_device, mesh=mesh, in_specs=placed, out_specs=P("ca", "tp"), check_vma=False
    )
```

```python
import functools
import math

import jax
import jax.numpy as jnp
import numpy as np
from jax import lax
from jax.experimental import pallas as pl
from jax.experimental.pallas import tpu as pltpu
from jax.sharding import PartitionSpec as P

GROUP = 4
HEAD_DIM = 128
REACH = 3
NY = 4
LAG = 3

rope_theta = 500000.0
logit_cap = 5.0

MESH = pl.DeviceIdType.MESH


def gather_kernel(
    nz,
    len_hbm, freq_hbm, x_hbm, wq_hbm, wk_hbm, wv_hbm,
    out_ref,
    xbuf, qbuf, kvbuf, accq, acckv, cosb, sinb, startb, win, query, acc, len_ref, freq_ref,
    loc_sem, qz_s, qz_r, qy_s, qy_r, qh_s, qh_r, kz_s, kz_r, ky_s, ky_r, h_s, h_r, qp_s, qp_r,
):
    n = nz * NY
    half = nz // 2
    rows = wq_hbm.shape[0]
    block = rows * NY
    hr = rows // 2
    c = lax.axis_index("ca")
    z, y = c // NY, c % NY
    zp = lax.rem(c + NY, n)
    zm = lax.rem(c + n - NY, n)
    yp = z * NY + lax.rem(y + 1, NY)
    ym = z * NY + lax.rem(y + NY - 1, NY)
    y2 = z * NY + lax.rem(y + 2, NY)
    cp1, cm1 = lax.rem(c + 1, n), lax.rem(c + n - 1, n)
    cp3, cm3 = lax.rem(c + REACH, n), lax.rem(c + n - REACH, n)
    partners = [zp, zm, yp, ym, y2, cp1, cm1, cp3, cm3]

    barrier = pltpu.get_barrier_semaphore()
    for other in partners:
        pl.semaphore_signal(barrier, inc=1, device_id={"ca": other}, device_id_type=MESH)

    off = [pl.multiple_of(rows * lax.rem(y + r, NY), rows) for r in range(NY)]

    def local(src, dst, i):
        return pltpu.make_async_copy(src, dst, loc_sem.at[i])

    own = pl.ds(off[0], rows)
    kw = wk_hbm.shape[1]
    cp_k = local(wk_hbm, kvbuf.at[0, own, pl.ds(0, kw)], 0)
    cp_v = local(wv_hbm, kvbuf.at[0, own, pl.ds(kw, kw)], 1)
    cp_q = local(wq_hbm, qbuf.at[0, own], 2)
    cp_x = local(x_hbm, xbuf, 3)
    cp_l = local(len_hbm, len_ref, 4)
    cp_f = local(freq_hbm, freq_ref, 5)
    for cp in (cp_k, cp_v, cp_q, cp_l, cp_f, cp_x):
        cp.start()

    def remote(src, dst, ssem, rsem, to):
        return pltpu.make_async_remote_copy(
            src_ref=src, dst_ref=dst, send_sem=ssem, recv_sem=rsem,
            device_id={"ca": to}, device_id_type=MESH,
        )

    def qz(s_from, s_to, d):
        return remote(
            qbuf.at[s_from, own], qbuf.at[s_to, own], qz_s.at[s_to], qz_r.at[s_to],
            zp if d == 0 else zm,
        )

    y_to = (yp, ym, y2)
    y_off = (3, 1, 2)

    def qy(kind, s, receiver=False):
        region = qbuf.at[s, pl.ds(off[y_off[kind] if receiver else 0], rows)]
        return remote(region, region, qy_s.at[kind, s], qy_r.at[kind, s], y_to[kind])

    def qh(kind, s, receiver=False):
        at = off[2] if receiver else off[y_off[kind]]
        region = qbuf.at[s, pl.ds(pl.multiple_of(at + kind * hr, hr), hr)]
        return remote(region, region, qh_s.at[kind, s], qh_r.at[kind, s], y_to[kind])

    def q_pass(s, further=lambda r: None):
        for kind in range(2):
            qy(kind, s, True).wait_recv()
            qh(kind, s).start()
            further(y_off[kind])

    def qp(s_from, s_to, r):
        region = pl.ds(off[r], rows)
        i = s_to - (half - 1)
        return remote(
            qbuf.at[s_from, region], qbuf.at[s_to, region], qp_s.at[i, r], qp_r.at[i, r],
            zp if s_to > s_from else zm,
        )

    def ky(kind, receiver=False):
        region = kvbuf.at[0, pl.ds(off[y_off[kind] if receiver else 0], rows)]
        return remote(region, region, ky_s.at[kind], ky_r.at[kind], y_to[kind])

    def kz(s_from, s_to, r, d):
        region = pl.ds(off[r], rows)
        return remote(
            kvbuf.at[s_from, region], kvbuf.at[s_to, region], kz_s.at[s_to, r], kz_r.at[s_to, r],
            zp if d == 0 else zm,
        )

    def columns(s):
        origin = lax.rem(z - s + nz, nz)
        return pl.ds(pl.multiple_of(origin * block, block), block)

    def product(buf, s):
        return jnp.dot(xbuf[:, columns(s)], buf[s], preferred_element_type=jnp.float32)

    def kz_pass(d, r, up_more, down_more):
        kz(d, d, r, 0).wait_recv()
        up_more(lambda: kz(d, d + 1, r, 0).start())
        kz(nz - d, nz - d, r, 1).wait_recv()
        down_more(lambda: kz(nz - d, nz - d - 1, r, 1).start())

    def q_ready(s):
        for kind in range(2):
            qh(kind, s, True).wait_recv()

    tok = x_hbm.shape[0]
    chunk = tok // half

    def prepare(i):
        at = pl.ds(pl.multiple_of(i * chunk, chunk), chunk)
        row = c * tok + i * chunk + lax.broadcasted_iota(jnp.int32, (chunk, HEAD_DIM), 0)
        start = jnp.zeros_like(row)
        end = jnp.int32(0)
        for doc in range(len_ref.shape[0]):
            end = end + len_ref[doc]
            start = jnp.where(row >= end, end, start)
        angle = (row - start).astype(jnp.float32) * freq_ref[0:1, :]
        lane = lax.broadcasted_iota(jnp.int32, (chunk, HEAD_DIM), 1)
        sine = jnp.sin(angle)
        cosb[at, :] = jnp.cos(angle)
        sinb[at, :] = jnp.where(lane < HEAD_DIM // 2, -sine, sine)
        startb[at, :] = start - (c - REACH) * tok

    pl.semaphore_wait(barrier, len(partners))

    cp_k.wait()
    cp_v.wait()
    for kind in range(3):
        ky(kind).start()
    kz(0, 1, 0, 0).start()
    kz(0, nz - 1, 0, 1).start()
    cp_q.wait()
    qz(0, 1, 0).start()
    qz(0, nz - 1, 1).start()
    for kind in range(2):
        qy(kind, 0).start()
    cp_l.wait()
    cp_f.wait()
    prepare(0)
    for kind in range(3):
        ky(kind, True).wait_recv()
        kz(0, 1, y_off[kind], 0).start()
        kz(0, nz - 1, y_off[kind], 1).start()
    cp_x.wait()
    acckv[...] = product(kvbuf, 0)

    def step(d, carry):
        up, down = d, nz - d
        always = lambda f: f()
        inner = pl.when(d < half - 1)

        kz_pass(d, 0, always, inner)
        qz(up, up, 0).wait_recv()
        qz(up, up + 1, 0).start()
        qz(down, down, 1).wait_recv()

        @inner
        def _():
            qz(down, down - 1, 1).start()

        @inner
        def _():
            for s in (up, down):
                for kind in range(2):
                    qy(kind, s).start()

        @pl.when(d > 1)
        def _():
            acckv[...] += product(kvbuf, up - 1) + product(kvbuf, down + 1)

        kz_pass(d, 3, always, inner)
        prepare(d)

        @pl.when(d == 1)
        def _():
            q_pass(0)

        @pl.when((d > 1) & (d < half - 1))
        def _():
            q_pass(up - 1)

        @pl.when(d == LAG)
        def _():
            q_ready(0)
            accq[...] = product(qbuf, 0)

        @pl.when(d > LAG)
        def _():
            q_ready(up - LAG)
            accq[...] += product(qbuf, up - LAG)

        kz_pass(d, 1, inner, always)

        @pl.when((d > 1) & (d < half - 1))
        def _():
            q_pass(down + 1)

        @pl.when(d > LAG)
        def _():
            q_ready(down + LAG)
            accq[...] += product(qbuf, down + LAG)

        kz_pass(d, 2, inner, always)
        return carry

    lax.fori_loop(1, half, step, 0)

    q_pass(half - 2, lambda r: qp(half - 2, half - 1, r).start())
    q_pass(half + 2, lambda r: qp(half + 2, half + 1, r).start())
    kz(half, half, 0, 0).wait_recv()
    acckv[...] += product(kvbuf, half - 1) + product(kvbuf, half + 1)
    cosine, sine_part = cosb[...], sinb[...]

    def rotated(values):
        return values * cosine + pltpu.roll(values, HEAD_DIM // 2, 1) * sine_part

    kz(half, half, 3, 0).wait_recv()
    kz(half, half, 1, 1).wait_recv()
    kz(half, half, 2, 1).wait_recv()
    total = acckv[...] + product(kvbuf, half)
    win[0, :, 0:HEAD_DIM] = rotated(total[:, :HEAD_DIM]).astype(jnp.bfloat16)
    win[0, :, HEAD_DIM:] = total[:, HEAD_DIM:].astype(jnp.bfloat16)

    upper, lower = pl.ds(0, tok // 2), pl.ds(tok // 2, tok // 2)

    def halo(i):
        src, dst, region, to = (
            (0, 1, upper, cp1), (0, 3, lower, cp3), (0, 1, lower, cp1), (0, 3, upper, cp3),
            (1, 2, upper, cp1), (3, 2, lower, cm1),
        )[i]
        return remote(win.at[src, region], win.at[dst, region], h_s.at[i], h_r.at[i], to)

    for i in range(4):
        halo(i).start()
    q_ready(half - 2)
    qp(half - 2, half - 1, 2).start()
    q_ready(half + 2)
    qp(half + 2, half + 1, 2).start()
    qp(half - 2, half - 1, 3).wait_recv()
    qp(half - 1, half, 3).start()
    qp(half + 2, half + 1, 1).wait_recv()
    qp(half + 1, half, 1).start()
    for d in range(half - LAG, half - 1):
        if d < half - 2:
            q_ready(d)
            q_ready(nz - d)
        accq[...] += product(qbuf, d) + product(qbuf, nz - d)
    halo(0).wait_recv()
    halo(4).start()
    halo(1).wait_recv()
    halo(5).start()
    qp(half + 2, half + 1, 2).wait_recv()
    qp(half + 1, half, 2).start()
    qp(half + 2, half + 1, 3).wait_recv()
    qp(half - 2, half - 1, 1).wait_recv()
    qp(half - 2, half - 1, 2).wait_recv()
    accq[...] += product(qbuf, half - 1) + product(qbuf, half + 1)
    qz(half, half, 0).wait_recv()
    qp(half - 1, half, 3).wait_recv()
    qp(half + 1, half, 1).wait_recv()
    qp(half + 1, half, 2).wait_recv()
    total = accq[...] + product(qbuf, half)
    for h in range(GROUP):
        part = slice(h * HEAD_DIM, (h + 1) * HEAD_DIM)
        query[:, part] = rotated(total[:, part]).astype(jnp.bfloat16)

    scale = 1.0 / (math.sqrt(HEAD_DIM) * logit_cap)
    gain = logit_cap * math.log2(math.e)

    def attend(r0, r_num, block, k0, k_num, own_keys=False):
        r, k = slice(r0, r0 + r_num), slice(k0, k0 + k_num)
        key = win[block, k, :HEAD_DIM]
        value = jnp.concatenate(
            [win[block, k, HEAD_DIM:], jnp.ones((k_num, HEAD_DIM), jnp.bfloat16)], axis=1
        )
        col = lax.broadcasted_iota(jnp.int32, (r_num, k_num), 1) + (REACH - block) * tok + k0
        start = startb[r, :]
        allowed = col >= jnp.concatenate([start] * (k_num // HEAD_DIM), axis=1)
        if own_keys:
            row = lax.broadcasted_iota(jnp.int32, (r_num, k_num), 0) + REACH * tok + r0
            allowed = allowed & (col <= row)
        for h in range(GROUP):
            raw = lax.dot_general(
                query[r, h * HEAD_DIM:(h + 1) * HEAD_DIM], key,
                (((1,), (1,)), ((), ())), preferred_element_type=jnp.float32,
            )
            weight = jnp.exp2(gain * jnp.tanh(raw * scale))
            weight = jnp.where(allowed, weight, 0.0).astype(jnp.bfloat16)
            part = jnp.dot(weight, value, preferred_element_type=jnp.float32)
            if own_keys:
                acc[h, r, :] = part
            else:
                acc[h, r, :] += part

    mid = tok // 2
    attend(0, mid, 0, 0, mid, True)
    attend(mid, mid, 0, 0, tok, True)

    halo(2).wait_recv()
    attend(0, tok, 1, 0, tok)
    halo(3).wait_recv()
    attend(0, mid, REACH, 0, tok)
    attend(mid, mid, REACH, mid, mid)
    halo(4).wait_recv()
    halo(5).wait_recv()
    attend(0, tok, 2, 0, tok)
    for h in range(GROUP):
        out_ref[:, h * HEAD_DIM:(h + 1) * HEAD_DIM] = (
            acc[h, :, :HEAD_DIM] / acc[h, :, HEAD_DIM:]
        ).astype(jnp.bfloat16)

    for i in range(6):
        halo(i).wait_send()
    for kind in range(3):
        ky(kind).wait_send()
    for s_from, s_to, pieces in (
        (half - 2, half - 1, (1, 2, 3)), (half + 2, half + 1, (1, 2, 3)),
        (half - 1, half, (3,)), (half + 1, half, (1, 2)),
    ):
        for r in pieces:
            qp(s_from, s_to, r).wait_send()

    def drain(s, carry):
        qz(s, s, 0).wait_send()
        for r in range(NY):
            kz(s, s, r, 0).wait_send()
        return carry

    lax.fori_loop(1, nz, drain, 0)

    def drain_y(s, carry):
        @pl.when((s < half - 1) | (s > half + 1))
        def _():
            for kind in range(2):
                qy(kind, s).wait_send()
                qh(kind, s).wait_send()

        return carry

    lax.fori_loop(0, nz, drain_y, 0)


def per_device(tokens, lengths, w_query, w_key, w_value):
    tok, depth = tokens.shape
    rows, q_width = w_query.shape
    kv_width = w_key.shape[1] + w_value.shape[1]
    nz = lax.axis_size("ca") // NY
    block = rows * NY
    half_dim = HEAD_DIM // 2
    frequency = rope_theta ** (-(np.arange(half_dim, dtype=np.float32) * 2.0) / HEAD_DIM)
    frequency = np.tile(np.concatenate([frequency, frequency]).astype(np.float32), (8, 1))

    hbm_spec = pl.BlockSpec(memory_space=pltpu.MemorySpace.HBM)
    vmem_spec = pl.BlockSpec(memory_space=pltpu.VMEM)
    dma = pltpu.SemaphoreType.DMA
    return pl.pallas_call(
        functools.partial(gather_kernel, nz),
        out_shape=jax.ShapeDtypeStruct((tok, q_width), jnp.bfloat16),
        in_specs=[hbm_spec] * 6,
        out_specs=vmem_spec,
        scratch_shapes=[
            pltpu.VMEM((tok, depth), jnp.bfloat16),
            pltpu.VMEM((nz, block, q_width), jnp.bfloat16),
            pltpu.VMEM((nz, block, kv_width), jnp.bfloat16),
            pltpu.VMEM((tok, q_width), jnp.float32),
            pltpu.VMEM((tok, kv_width), jnp.float32),
            pltpu.VMEM((tok, HEAD_DIM), jnp.float32),
            pltpu.VMEM((tok, HEAD_DIM), jnp.float32),
            pltpu.VMEM((tok, HEAD_DIM), jnp.int32),
            pltpu.VMEM((REACH + 1, tok, kv_width), jnp.bfloat16),
            pltpu.VMEM((tok, q_width), jnp.bfloat16),
            pltpu.VMEM((GROUP, tok, 2 * HEAD_DIM), jnp.float32),
            pltpu.SMEM(lengths.shape, jnp.int32),
            pltpu.VMEM(frequency.shape, jnp.float32),
            dma((6,)),
            dma((nz,)), dma((nz,)),
            dma((2, nz)), dma((2, nz)),
            dma((2, nz)), dma((2, nz)),
            dma((nz, NY)), dma((nz, NY)),
            dma((3,)), dma((3,)),
            dma((6,)), dma((6,)),
            dma((3, NY)), dma((3, NY)),
        ],
        compiler_params=pltpu.CompilerParams(
            collective_id=0, has_side_effects=True
        ),
        name="gather_project",
    )(lengths, jnp.asarray(frequency), tokens, w_query, w_key, w_value)


def solution(mesh):
    placed = (P("ca", None), P(), P("ca", "tp"), P("ca", "tp"), P("ca", "tp"))
    return jax.shard_map(
        per_device, mesh=mesh, in_specs=placed, out_specs=P("ca", "tp"), check_vma=False
    )
```
